32 devices in a mesh: section: 4 (over z), dp: 4 (over x, core), mp: 2 (over y).
Axes of the slice: x: 2, y: 2, z: 4, core: 2. Of those that a mesh axis runs over, the one named last changes fastest.
Arguments:
- tokens: bfloat16 [3, 16, 4096], P(None, ('dp', 'mp')), may hold values from -6 to 6
- member_ids: int32 [3, 16], replicated, may hold values from 0 to 3
- cotangent: bfloat16 [3, 16, 4096], P(None, ('dp', 'mp')), may hold values from -6 to 6
- w_gate: bfloat16 [4, 4096, 14336], P('section', None, ('dp', 'mp')), may hold values from -0.09375 to 0.09375
- w_up: bfloat16 [4, 4096, 14336], P('section', None, ('dp', 'mp')), may hold values from -0.09375 to 0.09375
- w_down: bfloat16 [4, 14336, 4096], P('section', ('dp', 'mp')), may hold values from -0.046875 to 0.046875
- in_scale: float32 [4, 4, 4096], P('section'), may hold values from 0.5 to 1.5
- mid_scale: float32 [4, 4, 14336], P('section', None, ('dp', 'mp')), may hold values from 0.5 to 1.5
- out_scale: float32 [4, 4, 4096], P('section'), may hold values from 0.5 to 1.5
- norm_gain: float32 [4, 4096], P('section'), may hold values from 0.5 to 1.5
Outputs:
- layer_outputs: bfloat16 [4, 3, 16, 4096], P('section', None, ('dp', 'mp'))
- section_in_grads: bfloat16 [4, 3, 16, 4096], P('section', None, ('dp', 'mp'))
- grad_gate: bfloat16 [4, 4096, 14336], P('section', None, ('dp', 'mp'))
- grad_up: bfloat16 [4, 4096, 14336], P('section', None, ('dp', 'mp'))
- grad_down: bfloat16 [4, 14336, 4096], P('section', ('dp', 'mp'))
- grad_in_scale: float32 [4, 4, 4096], P('section')
- grad_mid_scale: float32 [4, 4, 14336], P('section', None, ('dp', 'mp'))
- grad_out_scale: float32 [4, 4, 4096], P('section')
- grad_gain: float32 [4, 4096], P('section')
The draws below stay inside these ranges and needn't reach their ends.
All inputs are finite; a program needn't handle non-finite values.
Results may differ from the reference program's by a relative error of at most 0.038.
Values may be sent and summed in bfloat16 or wider, within the bound.
No kernel may reach another device: no remote copies, remote signals or barrier semaphores. Data moves between devices by JAX's collectives and lax.ppermute only.
A program may use at most 256 MiB of HBM per device.

```python
import jax
import jax.numpy as jnp
from jax import lax

D = 4096
FF = 14336
MEMBERS = 4
MICRO = 3
TOKENS_MB = 16
LAYERS = 4


def touch_ends(drawn, rng, least, top_value):
    longest = drawn.shape.index(max(drawn.shape))
    spots = []
    for shift in (0, 1):
        where = [jax.random.randint(jax.random.fold_in(rng, axis), (), 0, length) for axis, length in enumerate(drawn.shape)]
        where[longest] = (where[longest] + shift) % drawn.shape[longest]
        spots.append(tuple(where))
    return drawn.at[spots[0]].set(least).at[spots[1]].set(top_value)


def levels(key, shape, cuts, least, top_value):
    factor_of, own = 1.0, jax.random.fold_in(key, 6)
    for axis_at, blocks in cuts:
        draws = jnp.exp(jax.random.uniform(jax.random.fold_in(own, axis_at), (blocks,), jnp.float32, least / len(cuts), top_value / len(cuts)))
        factor_of = factor_of * jnp.repeat(draws, shape[axis_at] // blocks).reshape([-1 if axis == axis_at else 1 for axis in range(len(shape))])
    return factor_of


def bell_draw(key, dims, spread, reach, cuts=(), kind=jnp.bfloat16):
    result = jax.random.normal(key, dims, jnp.float32) * spread
    if len(cuts) > 0:
        result = levels(key, dims, cuts, -0.22, 0.18) * result
    return jnp.clip(result, min=-reach, max=reach).astype(kind)


def setup_inputs(seed: int = 0) -> dict:
    arg_keys = jax.random.split(jax.random.key(seed), 11)
    return {
        "tokens": bell_draw(arg_keys[0], (MICRO, TOKENS_MB, D), 1.0, 6.0, ((1, 8),)),
        "member_ids": touch_ends(jax.random.randint(arg_keys[1], (MICRO, TOKENS_MB), 0, MEMBERS), jax.random.fold_in(arg_keys[1], 1), 0, MEMBERS - 1).astype(jnp.int32),
        "cotangent": bell_draw(arg_keys[2], (MICRO, TOKENS_MB, D), 1.0, 6.0, ((1, 8),)),
        "w_gate": bell_draw(arg_keys[3], (LAYERS, D, FF), D ** -0.5, 0.09375, ((0, 4), (2, 8))),
        "w_up": bell_draw(arg_keys[4], (LAYERS, D, FF), D ** -0.5, 0.09375, ((0, 4), (2, 8))),
        "w_down": bell_draw(arg_keys[5], (LAYERS, FF, D), FF ** -0.5, 0.046875, ((0, 4), (1, 8))),
        "in_scale": jnp.clip(0.5 + 1.0 * jax.random.uniform(arg_keys[6], (LAYERS, MEMBERS, D), jnp.float32) ** levels(arg_keys[6], (LAYERS, MEMBERS, D), ((0, 4),), -0.2, 0.2), 0.5, 1.5),
        "mid_scale": jnp.clip(0.5 + 1.0 * jax.random.uniform(arg_keys[7], (LAYERS, MEMBERS, FF), jnp.float32) ** levels(arg_keys[7], (LAYERS, MEMBERS, FF), ((0, 4), (2, 8)), -0.2, 0.2), 0.5, 1.5),
        "out_scale": jnp.clip(0.5 + 1.0 * jax.random.uniform(arg_keys[8], (LAYERS, MEMBERS, D), jnp.float32) ** levels(arg_keys[8], (LAYERS, MEMBERS, D), ((0, 4),), -0.2, 0.2), 0.5, 1.5),
        "norm_gain": jnp.clip(1.0 + 0.1 * jax.random.normal(arg_keys[9], (LAYERS, D), jnp.float32), 0.5, 1.5),
    }


EPS = 1e-05
HIGH = lax.Precision.HIGHEST

def member_table(onehot, table):
    return jnp.dot(onehot, table, precision=HIGH)

def member_sums(onehot, values):
    return jnp.dot(onehot.T, values, precision=HIGH)

def contract_rows(left, right):
    return lax.dot_general(left, right, (((0,), (0,)), ((), ())), preferred_element_type=jnp.float32)

def contract_cols(left, right):
    return lax.dot_general(left, right, (((1,), (1,)), ((), ())), preferred_element_type=jnp.float32)

def reference(tokens, member_ids, cotangent, w_gate, w_up, w_down, in_scale, mid_scale, out_scale, norm_gain):
    layers = w_gate.shape[0]
    micro = tokens.shape[0]
    members = in_scale.shape[1]
    labels = jnp.arange(members, dtype=jnp.int32)
    hots = [(member_ids[k][:, None] == labels[None, :]).astype(jnp.float32) for k in range(micro)]
    saved = {}
    layer_outs = []
    for layer in range(layers):
        outs_here = []
        for k in range(micro):
            current = tokens[k] if layer == 0 else layer_outs[layer - 1][k]
            onehot = hots[k]
            x_float = current.astype(jnp.float32)
            inv_rms = lax.rsqrt(lax.optimization_barrier(jnp.mean(x_float * x_float, axis=-1, keepdims=True)) + EPS)
            normed = x_float * inv_rms
            scaled = (normed * norm_gain[layer] * member_table(onehot, in_scale[layer])).astype(jnp.bfloat16)
            gate_pre = jnp.dot(scaled, w_gate[layer], preferred_element_type=jnp.float32)
            up_pre = jnp.dot(scaled, w_up[layer], preferred_element_type=jnp.float32)
            product = jax.nn.silu(gate_pre) * up_pre
            hidden = (product * member_table(onehot, mid_scale[layer])).astype(jnp.bfloat16)
            down_out = jnp.dot(hidden, w_down[layer], preferred_element_type=jnp.float32)
            x_next = (x_float + down_out * member_table(onehot, out_scale[layer])).astype(jnp.bfloat16)
            saved[layer, k] = (x_float, inv_rms, normed, scaled, gate_pre, up_pre, product, hidden, down_out)
            outs_here.append(x_next)
        layer_outs.append(outs_here)
    grads_in = [None] * layers
    gates_acc, ups_acc, downs_acc = ([], [], [])
    in_acc, mid_acc, out_acc, gain_acc = ([], [], [], [])
    upper = [cotangent[k] for k in range(micro)]
    for layer in reversed(range(layers)):
        acc_gate = jnp.zeros(w_gate.shape[1:], jnp.float32)
        acc_up = jnp.zeros(w_up.shape[1:], jnp.float32)
        acc_down = jnp.zeros(w_down.shape[1:], jnp.float32)
        acc_in = jnp.zeros(in_scale.shape[1:], jnp.float32)
        acc_mid = jnp.zeros(mid_scale.shape[1:], jnp.float32)
        acc_out = jnp.zeros(out_scale.shape[1:], jnp.float32)
        acc_gain = jnp.zeros(norm_gain.shape[1:], jnp.float32)
        lower = []
        for k in range(micro):
            onehot = hots[k]
            x_float, inv_rms, normed, scaled, gate_pre, up_pre, product, hidden, down_out = saved[layer, k]
            grad_y = upper[k].astype(jnp.float32)
            acc_out = acc_out + member_sums(onehot, grad_y * down_out)
            scaled_cot = (grad_y * member_table(onehot, out_scale[layer])).astype(jnp.bfloat16)
            grad_hidden = contract_cols(scaled_cot, w_down[layer])
            acc_down = acc_down + contract_rows(hidden, scaled_cot)
            acc_mid = acc_mid + member_sums(onehot, grad_hidden * product)
            grad_product = grad_hidden * member_table(onehot, mid_scale[layer])
            sigma = jax.nn.sigmoid(gate_pre)
            grad_gate_pre = (grad_product * up_pre * sigma * (1.0 + gate_pre * (1.0 - sigma))).astype(jnp.bfloat16)
            grad_up_pre = (grad_product * gate_pre * sigma).astype(jnp.bfloat16)
            acc_gate = acc_gate + contract_rows(scaled, grad_gate_pre)
            acc_up = acc_up + contract_rows(scaled, grad_up_pre)
            grad_scaled = contract_cols(grad_gate_pre, w_gate[layer]) + contract_cols(grad_up_pre, w_up[layer])
            acc_in = acc_in + member_sums(onehot, grad_scaled * normed * norm_gain[layer])
            grad_w = grad_scaled * member_table(onehot, in_scale[layer])
            acc_gain = acc_gain + lax.optimization_barrier(jnp.sum(grad_w * normed, axis=0))
            grad_normed = grad_w * norm_gain[layer]
            grad_x = inv_rms * (grad_normed - normed * lax.optimization_barrier(jnp.mean(grad_normed * normed, axis=-1, keepdims=True)))
            lower.append((grad_y + grad_x).astype(jnp.bfloat16))
        grads_in[layer] = jnp.stack(lower)
        upper = lower
        gates_acc.insert(0, acc_gate.astype(jnp.bfloat16))
        ups_acc.insert(0, acc_up.astype(jnp.bfloat16))
        downs_acc.insert(0, acc_down.astype(jnp.bfloat16))
        in_acc.insert(0, acc_in)
        mid_acc.insert(0, acc_mid)
        out_acc.insert(0, acc_out)
        gain_acc.insert(0, acc_gain)
    layer_outputs = jnp.stack([jnp.stack(layer_outs[layer]) for layer in range(layers)])
    return (layer_outputs, jnp.stack(grads_in), jnp.stack(gates_acc), jnp.stack(ups_acc), jnp.stack(downs_acc), jnp.stack(in_acc), jnp.stack(mid_acc), jnp.stack(out_acc), jnp.stack(gain_acc))
```

```python
import jax
import jax.numpy as jnp
from jax import lax
from jax.experimental import pallas as pl
from jax.experimental.pallas import tpu as pltpu
from jax.sharding import PartitionSpec as P

EPS = 1e-05
HIGH = lax.Precision.HIGHEST
GROUP = ("dp", "mp")


def group_size():
    return lax.axis_size("dp") * lax.axis_size("mp")


def core_offset():
    return lax.axis_size("mp")


def chip_offsets():
    return [j for j in range(group_size()) if not j & core_offset()]


def slot_offsets():
    return chip_offsets() + [j | core_offset() for j in chip_offsets()]


def swapped(block, offset):
    route = [(i, i ^ offset) for i in range(group_size())]
    return lax.ppermute(block, GROUP, route)


def join_kernel(*refs):
    parts, out, stacked = refs[:-2], refs[-2], refs[-1]
    rows = parts[0].shape[0]
    for k, part in enumerate(parts):
        stacked[k * rows : (k + 1) * rows, :] = part[...].astype(jnp.float32)
    out[...] = stacked[...].astype(out.dtype)


def join(parts):
    rows, width = parts[0].shape
    shape = (rows * len(parts), width)
    return pl.pallas_call(
        join_kernel,
        out_shape=jax.ShapeDtypeStruct(shape, parts[0].dtype),
        scratch_shapes=[pltpu.VMEM(shape, jnp.float32)],
        compiler_params=pltpu.CompilerParams(vmem_limit_bytes=(1 << 21) + 16 * shape[0] * width),
        name="join",
    )(*parts)


def crossed(parts):
    pair = join(parts)
    return pair, swapped(pair, core_offset())


def spread(block):
    return crossed([block] + [swapped(block, j) for j in chip_offsets()[1:]])


def spread_along(block, distance):
    sections = lax.axis_size("section")
    count = group_size()
    parts = []
    for j in chip_offsets():
        route = [
            (s * count + i, (s + distance) * count + (i ^ j))
            for s in range(sections)
            if 0 <= s + distance < sections
            for i in range(count)
        ]
        parts.append(lax.ppermute(block, ("section",) + GROUP, route))
    return crossed(parts), parts[0]


def row_sums(kept, sent, rows):
    pair = kept + swapped(sent, core_offset()).astype(jnp.float32)
    part = pair.astype(jnp.bfloat16)
    total = pair[:rows]
    for k, j in enumerate(chip_offsets()):
        if j:
            total = total + swapped(part[k * rows : (k + 1) * rows], j).astype(jnp.float32)
    return total


def chunk_of(hidden):
    return 256 if hidden % 256 == 0 else hidden


def dot(left, right):
    return jnp.dot(left, right, preferred_element_type=jnp.float32)


def add_to(total, part, start):
    if start:
        total[...] = part
    else:
        total[...] += part


def choose(flag, first, arriving, whole):
    half = first[0].shape[0]
    for k in range(2):
        here = jnp.where(
            flag[0] > 0, first[k][...].astype(jnp.float32), arriving[k][...].astype(jnp.float32)
        )
        whole[k * half : (k + 1) * half, :] = here


def hand_out(total, kept, sent):
    half = kept.shape[0]
    kept[...] = total[:half]
    sent[...] = total[half:].astype(jnp.bfloat16)


class Weights:
    def __init__(self, refs, axes):
        self.refs, self.axes = refs, axes

    def at(self, k, s):
        ref = self.refs[k]
        return ref.at[:, s] if self.axes[k] else ref.at[s, :]


def fetches(sources, kept, axes, chunks, sems):
    src, dst = Weights(sources, axes), Weights(kept, axes)
    return [
        [pltpu.make_async_copy(src.at(k, s), dst.at(k, s), sems.at[k, i]) for k in range(3)]
        for i, s in enumerate(chunks)
    ]


def chunks_of(hidden):
    size = chunk_of(hidden)
    return [slice(i * size, (i + 1) * size) for i in range(hidden // size)]


FORWARD_AXES = (1, 1, 0)
BACKWARD_AXES = (0, 0, 1)


def forward_kernel(*refs, load, turn, keep):
    refs = list(refs)
    flag, first, arriving, gain, in_tok, mid = refs[0], refs[1:3], refs[3:5], *refs[5:8]
    given = refs[8:11]
    refs = refs[11:]
    kept_out, sent_out = refs[:2]
    refs = refs[2:]
    if load:
        weights, refs = refs[:3], refs[3:]
    else:
        weights = given
    if turn is not None:
        turned, refs = refs[0], refs[1:]
    if keep:
        gate_out, up_out, hidden_out, scaled_out = refs[:4]
        refs = refs[4:]
    total, scaled, refs = refs[0], refs[1], refs[2:]
    chunks = chunks_of(mid.shape[1])
    if load:
        copies = fetches(given, weights, FORWARD_AXES, chunks, refs[0])
        for group in copies:
            for copy in group:
                copy.start()
    choose(flag, first, arriving, total)
    x_whole = total[...]
    inv_rms = lax.rsqrt(jnp.mean(x_whole * x_whole, axis=-1, keepdims=True) + EPS)
    scaled[...] = (x_whole * inv_rms * gain[...] * in_tok[...]).astype(jnp.bfloat16)
    if keep:
        scaled_out[...] = scaled[...]
    if turn is not None:
        staged, sems = refs[-2:]
    gate_w, up_w, down_w = weights
    writes = []
    for i, s in enumerate(chunks):
        if load:
            copies[i][0].wait()
            copies[i][1].wait()
        gate = dot(scaled[...], gate_w[:, s])
        up = dot(scaled[...], up_w[:, s])
        hidden = (gate / (1.0 + jnp.exp(-gate)) * up * mid[:, s]).astype(jnp.bfloat16)
        if keep:
            gate_out[:, s] = gate
            up_out[:, s] = up
            hidden_out[:, s] = hidden
        if turn is not None:
            slot = i % 2
            if i >= 2:
                writes[i - 2].wait()
            if turn < 2:
                staged[slot] = weights[turn][:, s].T
                target = turned.at[s, :]
            else:
                staged[slot] = weights[turn][s, :].T
                target = turned.at[:, s]
            write = pltpu.make_async_copy(staged.at[slot], target, sems.at[slot])
            write.start()
            writes.append(write)
        if load:
            copies[i][2].wait()
        add_to(total, dot(hidden, down_w[s, :]), i == 0)
    hand_out(total, kept_out, sent_out)
    for write in writes[-2:]:
        write.wait()


def placed(weights, load):
    space = pltpu.HBM if load else pltpu.VMEM
    return [pltpu.with_memory_space_constraint(w, space) for w in weights]


def grant(tall, width):
    return (10 << 20) + 22 * tall * width


def specs(count, space):
    return [pl.BlockSpec(memory_space=space)] * count


def forward_stage(flag, first, arriving, gain, in_tok, mid, weights, load, turn, keep):
    tall, width = in_tok.shape
    hidden = mid.shape[1]
    size = chunk_of(hidden)
    out = [
        jax.ShapeDtypeStruct((tall // 2, width), jnp.float32),
        jax.ShapeDtypeStruct((tall // 2, width), jnp.bfloat16),
    ]
    out_specs = specs(2, pltpu.VMEM)
    scratch = [pltpu.VMEM((tall, width), t) for t in (jnp.float32, jnp.bfloat16)]
    if load:
        out += [pltpu.VMEM(w.shape, w.dtype) for w in weights]
        out_specs += specs(3, pltpu.VMEM)
        scratch.append(pltpu.SemaphoreType.DMA((3, hidden // size)))
    if turn is not None:
        out.append(pltpu.HBM(weights[turn].shape[::-1], jnp.bfloat16))
        out_specs += specs(1, pltpu.HBM)
        block = (size, width) if turn < 2 else (width, size)
        scratch += [pltpu.VMEM((2,) + block, jnp.bfloat16), pltpu.SemaphoreType.DMA((2,))]
    if keep:
        kinds = (jnp.float32, jnp.float32, jnp.bfloat16)
        out += [jax.ShapeDtypeStruct((tall, hidden), t) for t in kinds]
        out.append(jax.ShapeDtypeStruct((tall, width), jnp.bfloat16))
        out_specs += specs(4, pltpu.VMEM)
    found = pl.pallas_call(
        lambda *refs: forward_kernel(*refs, load=load, turn=turn, keep=keep),
        in_specs=specs(1, pltpu.SMEM) + specs(7, pltpu.VMEM) + specs(3, pltpu.HBM if load else pltpu.VMEM),
        out_specs=out_specs,
        out_shape=out,
        scratch_shapes=scratch,
        compiler_params=pltpu.CompilerParams(vmem_limit_bytes=grant(tall, width)),
        name=f"forward_{int(load)}{-1 if turn is None else turn}{int(keep)}",
    )(flag, *first, *arriving, gain, in_tok, mid, *placed(weights, load))
    return found


def backward_kernel(*refs, load, keep):
    refs = list(refs)
    flag, last, arriving, out_tok, mid, silu_grad, silu_gate = refs[0], refs[1:3], refs[3:5], *refs[5:9]
    given = refs[9:12]
    kept_out, sent_out = refs[12:14]
    refs = refs[14:]
    if load:
        weights, refs = refs[:3], refs[3:]
    else:
        weights = given
    if keep:
        hidden_out, gate_out, up_out, cot_out = refs[:4]
        refs = refs[4:]
    total, cot = refs[:2]
    chunks = chunks_of(mid.shape[1])
    if load:
        copies = fetches(given, weights, BACKWARD_AXES, chunks, refs[2])
        for group in copies:
            for k in (2, 0, 1):
                group[k].start()
    choose(flag, last, arriving, total)
    cot[...] = (total[...] * out_tok[...]).astype(jnp.bfloat16)
    if keep:
        cot_out[...] = cot[...]
    gate_w, up_w, down_w = weights
    for i, s in enumerate(chunks):
        if load:
            copies[i][2].wait()
        grad_hidden = dot(cot[...], down_w[:, s])
        grad_product = grad_hidden * mid[:, s]
        grad_gate = (grad_product * silu_grad[:, s]).astype(jnp.bfloat16)
        grad_up = (grad_product * silu_gate[:, s]).astype(jnp.bfloat16)
        if keep:
            hidden_out[:, s] = grad_hidden
            gate_out[:, s] = grad_gate
            up_out[:, s] = grad_up
        if load:
            copies[i][0].wait()
            copies[i][1].wait()
        add_to(total, dot(grad_gate, gate_w[s, :]) + dot(grad_up, up_w[s, :]), i == 0)
    hand_out(total, kept_out, sent_out)


def backward_stage(flag, last, arriving, tables, weights, load, keep):
    out_tok, mid = tables[:2]
    tall, width = out_tok.shape
    hidden = mid.shape[1]
    out = [
        jax.ShapeDtypeStruct((tall // 2, width), jnp.float32),
        jax.ShapeDtypeStruct((tall // 2, width), jnp.bfloat16),
    ]
    out_specs = specs(2, pltpu.VMEM)
    scratch = [pltpu.VMEM((tall, width), t) for t in (jnp.float32, jnp.bfloat16)]
    if load:
        out += [pltpu.VMEM(w.shape, w.dtype) for w in weights]
        out_specs += specs(3, pltpu.VMEM)
        scratch.append(pltpu.SemaphoreType.DMA((3, hidden // chunk_of(hidden))))
    if keep:
        kinds = (jnp.float32, jnp.bfloat16, jnp.bfloat16)
        out += [jax.ShapeDtypeStruct((tall, hidden), t) for t in kinds]
        out.append(jax.ShapeDtypeStruct((tall, width), jnp.bfloat16))
        out_specs += specs(4, pltpu.VMEM)
    return pl.pallas_call(
        lambda *refs: backward_kernel(*refs, load=load, keep=keep),
        in_specs=specs(1, pltpu.SMEM) + specs(8, pltpu.VMEM) + specs(3, pltpu.HBM if load else pltpu.VMEM),
        out_specs=out_specs,
        out_shape=out,
        scratch_shapes=scratch,
        compiler_params=pltpu.CompilerParams(vmem_limit_bytes=grant(tall, width)),
        name=f"backward_{int(load)}{int(keep)}",
    )(flag, *last, *arriving, *tables, *placed(weights, load))


def member_table(onehot, table):
    return jnp.dot(onehot, table, precision=HIGH)


def member_sums(onehot, values):
    return jnp.dot(onehot.T, values, precision=HIGH)


def contract_rows(left, right):
    return lax.dot_general(
        left, right, (((0,), (0,)), ((), ())), preferred_element_type=jnp.float32
    )


def on_device(
    tokens, member_ids, cotangent, w_gate, w_up, w_down, in_scale, mid_scale, out_scale, norm_gain
):
    sections = lax.axis_size("section")
    section = lax.axis_index("section")
    micro, own, width = tokens.shape
    rows = micro * own
    count = group_size()
    group = lax.axis_index("dp") * lax.axis_size("mp") + lax.axis_index("mp")
    gate_w, up_w, down_w = w_gate[0], w_up[0], w_down[0]
    in_tab, mid_tab, out_tab = in_scale[0], mid_scale[0], out_scale[0]
    gain = norm_gain[0]
    members = in_tab.shape[0]
    labels = jnp.arange(members, dtype=jnp.int32)
    owners = jnp.bitwise_xor(group, jnp.array(slot_offsets(), jnp.int32))
    by_owner = member_ids.reshape(micro, count, own).transpose(1, 0, 2).reshape(count, rows)
    ids = jnp.take(by_owner, owners, axis=0).reshape(count * rows)
    full_hot = (ids[:, None] == labels[None, :]).astype(jnp.float32)
    row_hot = full_hot[:rows]
    in_tok = member_table(full_hot, in_tab)
    out_tok = member_table(full_hot, out_tab)
    mid_tok = member_table(full_hot, mid_tab)
    own_first = tokens.reshape(rows, width)
    own_last = cotangent.reshape(rows, width)
    start_flag = (section == 0).astype(jnp.int32)[None]
    end_flag = (section == sections - 1).astype(jnp.int32)[None]
    ready = (full_hot, row_hot, in_tok, out_tok, mid_tok, own_first, own_last, start_flag, end_flag)
    full_hot, row_hot, in_tok, out_tok, mid_tok, own_first, own_last, start_flag, end_flag = (
        lax.optimization_barrier(ready)
    )
    out_rows = out_tok[:rows]
    first = spread(own_first)
    last = spread(own_last)
    gain_row = gain[None]

    at_start = start_flag[0] > 0
    arriving, part = first, own_first
    weights = (gate_w, up_w, down_w)
    turned = [None] * 3
    for step in range(sections):
        keep = step + 1 == sections
        turn = step - 1 if 0 < step <= 3 else None
        kept, sent, *found = forward_stage(
            start_flag, first, arriving, gain_row, in_tok, mid_tok, weights, step == 0, turn, keep
        )
        if step == 0:
            weights, found = found[:3], found[3:]
        if turn is not None:
            turned[turn], found = found[0], found[1:]
        if keep:
            gate_pre, up_pre, hidden, whole_scaled = found
        x_own = jnp.where(at_start, own_first, part).astype(jnp.float32)
        down_out = row_sums(kept, sent, rows)
        x_next = (x_own + down_out * out_rows).astype(jnp.bfloat16)
        if step + 1 < sections:
            arriving, part = spread_along(x_next, 1)

    turned = [w.T if t is None else t for w, t in zip((gate_w, up_w, down_w), turned)]
    inv_rms = lax.rsqrt(jnp.mean(x_own * x_own, axis=-1, keepdims=True) + EPS)
    normed = x_own * inv_rms
    in_rows = in_tok[:rows]
    product = jax.nn.silu(gate_pre) * up_pre
    sigma = jax.nn.sigmoid(gate_pre)
    silu_gate = gate_pre * sigma
    silu_grad = up_pre * sigma * (1.0 + gate_pre * (1.0 - sigma))
    tables = (out_tok, mid_tok, silu_grad, silu_gate)
    at_end = end_flag[0] > 0
    arriving, part = last, own_last
    for step in range(sections):
        keep = step + 1 == sections
        kept, sent, *found = backward_stage(end_flag, last, arriving, tables, turned, step == 0, keep)
        if step == 0:
            turned, found = found[:3], found[3:]
        if keep:
            grad_hidden, grad_gate_pre, grad_up_pre, whole_cot = found
        grad_y = jnp.where(at_end, own_last, part).astype(jnp.float32)
        grad_scaled = row_sums(kept, sent, rows)
        grad_w = grad_scaled * in_rows
        grad_normed = grad_w * gain
        grad_x = inv_rms * (
            grad_normed - normed * jnp.mean(grad_normed * normed, axis=-1, keepdims=True)
        )
        grad_input = (grad_y + grad_x).astype(jnp.bfloat16)
        if step + 1 < sections:
            arriving, part = spread_along(grad_input, -1)

    acc_out = member_sums(row_hot, grad_y * down_out)
    acc_in = member_sums(row_hot, grad_scaled * normed * gain)
    acc_gain = jnp.sum(grad_w * normed, axis=0)
    small = jnp.concatenate([acc_in, acc_out, acc_gain[None]], 0)
    small = row_sums_all(small)
    acc_mid = member_sums(full_hot, grad_hidden * product)
    acc_gate = contract_rows(whole_scaled, grad_gate_pre)
    acc_up = contract_rows(whole_scaled, grad_up_pre)
    acc_down = contract_rows(hidden, whole_cot)
    return (
        x_next.reshape(1, micro, own, width),
        grad_input.reshape(1, micro, own, width),
        acc_gate.astype(jnp.bfloat16)[None],
        acc_up.astype(jnp.bfloat16)[None],
        acc_down.astype(jnp.bfloat16)[None],
        small[None, :members],
        acc_mid[None],
        small[None, members : 2 * members],
        small[None, 2 * members],
    )


def row_sums_all(small):
    total = small.astype(jnp.bfloat16)
    offset = 1
    while offset < group_size():
        total = total.astype(jnp.float32) + swapped(total, offset).astype(jnp.float32)
        offset *= 2
        if offset < group_size():
            total = total.astype(jnp.bfloat16)
    return total


def solution(mesh):
    in_specs = (
        P(None, ("dp", "mp"), None),
        P(),
        P(None, ("dp", "mp"), None),
        P("section", None, ("dp", "mp")),
        P("section", None, ("dp", "mp")),
        P("section", ("dp", "mp"), None),
        P("section", None, None),
        P("section", None, ("dp", "mp")),
        P("section", None, None),
        P("section", None),
    )
    out_specs = (
        P("section", None, ("dp", "mp"), None),
        P("section", None, ("dp", "mp"), None),
        P("section", None, ("dp", "mp")),
        P("section", None, ("dp", "mp")),
        P("section", ("dp", "mp"), None),
        P("section", None, None),
        P("section", None, ("dp", "mp")),
        P("section", None, None),
        P("section", None),
    )
    return jax.shard_map(
        on_device, mesh=mesh, in_specs=in_specs, out_specs=out_specs, check_vma=False
    )
```

```python
import jax
import jax.numpy as jnp
from jax import lax
from jax.experimental import pallas as pl
from jax.experimental.pallas import tpu as pltpu
from jax.sharding import PartitionSpec as P

EPS = 1e-05
HIGH = lax.Precision.HIGHEST
GROUP = ("dp", "mp")


def group_size():
    return lax.axis_size("dp") * lax.axis_size("mp")


def core_offset():
    return lax.axis_size("mp")


def chip_offsets():
    return [j for j in range(group_size()) if not j & core_offset()]


def slot_offsets():
    return chip_offsets() + [j | core_offset() for j in chip_offsets()]


def swapped(block, offset):
    route = [(i, i ^ offset) for i in range(group_size())]
    return lax.ppermute(block, GROUP, route)


def join_kernel(*refs):
    parts, out, stacked = refs[:-2], refs[-2], refs[-1]
    rows = parts[0].shape[0]
    for k, part in enumerate(parts):
        stacked[k * rows : (k + 1) * rows, :] = part[...].astype(jnp.float32)
    out[...] = stacked[...].astype(out.dtype)


def join(parts):
    rows, width = parts[0].shape
    shape = (rows * len(parts), width)
    return pl.pallas_call(
        join_kernel,
        out_shape=jax.ShapeDtypeStruct(shape, parts[0].dtype),
        scratch_shapes=[pltpu.VMEM(shape, jnp.float32)],
        compiler_params=pltpu.CompilerParams(vmem_limit_bytes=(1 << 21) + 16 * shape[0] * width),
        name="join",
    )(*parts)


def crossed(parts):
    pair = join(parts)
    return pair, swapped(pair, core_offset())


def spread(block):
    return crossed([block] + [swapped(block, j) for j in chip_offsets()[1:]])


def spread_along(block, distance):
    count = lax.axis_size("section")
    route = [(i, i + distance) for i in range(count) if 0 <= i + distance < count]
    arrived = lax.ppermute(block, "section", route)
    return spread(arrived), arrived


def row_sums(kept, sent, rows):
    pair = kept + swapped(sent, core_offset()).astype(jnp.float32)
    part = pair.astype(jnp.bfloat16)
    total = pair[:rows]
    for k, j in enumerate(chip_offsets()):
        if j:
            total = total + swapped(part[k * rows : (k + 1) * rows], j).astype(jnp.float32)
    return total


def chunk_of(hidden):
    return 256 if hidden % 256 == 0 else hidden


def dot(left, right):
    return jnp.dot(left, right, preferred_element_type=jnp.float32)


def choose(flag, first, arriving, whole):
    half = first[0].shape[0]
    for k in range(2):
        here = jnp.where(
            flag[0] > 0, first[k][...].astype(jnp.float32), arriving[k][...].astype(jnp.float32)
        )
        whole[k * half : (k + 1) * half, :] = here


def hand_out(total, kept, sent):
    half = kept.shape[0]
    kept[...] = total[:half]
    sent[...] = total[half:].astype(jnp.bfloat16)


def fetches(sources, kept, axes, i, s, sems):
    return [
        pltpu.make_async_copy(
            src.at[:, s] if axis else src.at[s, :],
            dst.at[:, s] if axis else dst.at[s, :],
            sems.at[k, i],
        )
        for k, (src, dst, axis) in enumerate(zip(sources, kept, axes))
    ]


def chunk_at(i, size):
    return pl.ds(pl.multiple_of(i * size, size), size)


def each_chunk(hidden, body, unroll):
    size = chunk_of(hidden)
    if unroll:
        for i in range(hidden // size):
            body(i, slice(i * size, (i + 1) * size))
        return

    def step(i, carry):
        body(i, chunk_at(i, size))
        return carry

    lax.fori_loop(0, hidden // size, step, 0)


FORWARD_AXES = (1, 1, 0)
BACKWARD_AXES = (0, 0, 1)


def forward_kernel(*refs, load, turn, keep):
    refs = list(refs)
    flag, first, arriving, gain, in_tok, mid = refs[0], refs[1:3], refs[3:5], *refs[5:8]
    given = refs[8:11]
    refs = refs[11:]
    kept_out, sent_out = refs[:2]
    refs = refs[2:]
    if load:
        weights, refs = refs[:3], refs[3:]
    else:
        weights = given
    if turn is not None:
        turned, refs = refs[0], refs[1:]
    if keep:
        gate_out, up_out, hidden_out, scaled_out = refs[:4]
        refs = refs[4:]
    total, scaled, refs = refs[0], refs[1], refs[2:]
    width = mid.shape[1]
    if load:

        def begin(i, s):
            for copy in fetches(given, weights, FORWARD_AXES, i, s, refs[0]):
                copy.start()

        each_chunk(width, begin, False)
    choose(flag, first, arriving, total)
    x_whole = total[...]
    inv_rms = lax.rsqrt(jnp.mean(x_whole * x_whole, axis=-1, keepdims=True) + EPS)
    scaled[...] = (x_whole * inv_rms * gain[...] * in_tok[...]).astype(jnp.bfloat16)
    if keep:
        scaled_out[...] = scaled[...]
    total[...] = jnp.zeros_like(total)
    gate_w, up_w, down_w = weights
    if turn is not None:
        staged, sems = refs[-2:]
        size = chunk_of(width)
        slices = [slice(i * size, (i + 1) * size) for i in range(width // size)]

        def written(i, s):
            target = turned.at[s, :] if turn < 2 else turned.at[:, s]
            return pltpu.make_async_copy(staged.at[i % 2], target, sems.at[i % 2])

    def step(i, s):
        if load:
            copies = fetches(given, weights, FORWARD_AXES, i, s, refs[0])
            copies[0].wait()
            copies[1].wait()
        gate = dot(scaled[...], gate_w[:, s])
        up = dot(scaled[...], up_w[:, s])
        hidden = (gate / (1.0 + jnp.exp(-gate)) * up * mid[:, s]).astype(jnp.bfloat16)
        if keep:
            gate_out[:, s] = gate
            up_out[:, s] = up
            hidden_out[:, s] = hidden
        if turn is not None:

            if i >= 2:
                written(i - 2, slices[i - 2]).wait()
            block = weights[turn][:, s] if turn < 2 else weights[turn][s, :]
            staged[i % 2] = block.T
            written(i, s).start()
        if load:
            copies[2].wait()
        total[...] += dot(hidden, down_w[s, :])

    each_chunk(width, step, not load)
    hand_out(total, kept_out, sent_out)
    if turn is not None:
        for i in range(max(0, len(slices) - 2), len(slices)):
            written(i, slices[i]).wait()


def placed(weights, load):
    space = pltpu.HBM if load else pltpu.VMEM
    return [pltpu.with_memory_space_constraint(w, space) for w in weights]


def grant(tall, width):
    return (10 << 20) + 22 * tall * width


def specs(count, space):
    return [pl.BlockSpec(memory_space=space)] * count


def forward_stage(flag, first, arriving, gain, in_tok, mid, weights, load, turn, keep):
    tall, width = in_tok.shape
    hidden = mid.shape[1]
    size = chunk_of(hidden)
    out = [
        jax.ShapeDtypeStruct((tall // 2, width), jnp.float32),
        jax.ShapeDtypeStruct((tall // 2, width), jnp.bfloat16),
    ]
    out_specs = specs(2, pltpu.VMEM)
    scratch = [pltpu.VMEM((tall, width), t) for t in (jnp.float32, jnp.bfloat16)]
    if load:
        out += [pltpu.VMEM(w.shape, w.dtype) for w in weights]
        out_specs += specs(3, pltpu.VMEM)
        scratch.append(pltpu.SemaphoreType.DMA((3, hidden // size)))
    if turn is not None:
        out.append(pltpu.HBM(weights[turn].shape[::-1], jnp.bfloat16))
        out_specs += specs(1, pltpu.HBM)
        block = (size, width) if turn < 2 else (width, size)
        scratch += [pltpu.VMEM((2,) + block, jnp.bfloat16), pltpu.SemaphoreType.DMA((2,))]
    if keep:
        kinds = (jnp.float32, jnp.float32, jnp.bfloat16)
        out += [jax.ShapeDtypeStruct((tall, hidden), t) for t in kinds]
        out.append(jax.ShapeDtypeStruct((tall, width), jnp.bfloat16))
        out_specs += specs(4, pltpu.VMEM)
    found = pl.pallas_call(
        lambda *refs: forward_kernel(*refs, load=load, turn=turn, keep=keep),
        in_specs=specs(1, pltpu.SMEM) + specs(7, pltpu.VMEM) + specs(3, pltpu.HBM if load else pltpu.VMEM),
        out_specs=out_specs,
        out_shape=out,
        scratch_shapes=scratch,
        compiler_params=pltpu.CompilerParams(vmem_limit_bytes=grant(tall, width)),
        name=f"forward_{int(load)}{-1 if turn is None else turn}{int(keep)}",
    )(flag, *first, *arriving, gain, in_tok, mid, *placed(weights, load))
    return found


def backward_kernel(*refs, load, keep):
    refs = list(refs)
    flag, last, arriving, out_tok, mid, silu_grad, silu_gate = refs[0], refs[1:3], refs[3:5], *refs[5:9]
    given = refs[9:12]
    kept_out, sent_out = refs[12:14]
    refs = refs[14:]
    if load:
        weights, refs = refs[:3], refs[3:]
    else:
        weights = given
    if keep:
        hidden_out, gate_out, up_out, cot_out = refs[:4]
        refs = refs[4:]
    total, cot = refs[:2]
    width = mid.shape[1]
    if load:

        def begin(i, s):
            copies = fetches(given, weights, BACKWARD_AXES, i, s, refs[2])
            for k in (2, 0, 1):
                copies[k].start()

        each_chunk(width, begin, False)
    choose(flag, last, arriving, total)
    cot[...] = (total[...] * out_tok[...]).astype(jnp.bfloat16)
    if keep:
        cot_out[...] = cot[...]
    total[...] = jnp.zeros_like(total)
    gate_w, up_w, down_w = weights

    def step(i, s):
        if load:
            copies = fetches(given, weights, BACKWARD_AXES, i, s, refs[2])
            copies[2].wait()
        grad_hidden = dot(cot[...], down_w[:, s])
        grad_product = grad_hidden * mid[:, s]
        grad_gate = (grad_product * silu_grad[:, s]).astype(jnp.bfloat16)
        grad_up = (grad_product * silu_gate[:, s]).astype(jnp.bfloat16)
        if keep:
            hidden_out[:, s] = grad_hidden
            gate_out[:, s] = grad_gate
            up_out[:, s] = grad_up
        if load:
            copies[0].wait()
            copies[1].wait()
        total[...] += dot(grad_gate, gate_w[s, :]) + dot(grad_up, up_w[s, :])

    each_chunk(width, step, not load)
    hand_out(total, kept_out, sent_out)


def backward_stage(flag, last, arriving, tables, weights, load, keep):
    out_tok, mid = tables[:2]
    tall, width = out_tok.shape
    hidden = mid.shape[1]
    out = [
        jax.ShapeDtypeStruct((tall // 2, width), jnp.float32),
        jax.ShapeDtypeStruct((tall // 2, width), jnp.bfloat16),
    ]
    out_specs = specs(2, pltpu.VMEM)
    scratch = [pltpu.VMEM((tall, width), t) for t in (jnp.float32, jnp.bfloat16)]
    if load:
        out += [pltpu.VMEM(w.shape, w.dtype) for w in weights]
        out_specs += specs(3, pltpu.VMEM)
        scratch.append(pltpu.SemaphoreType.DMA((3, hidden // chunk_of(hidden))))
    if keep:
        kinds = (jnp.float32, jnp.bfloat16, jnp.bfloat16)
        out += [jax.ShapeDtypeStruct((tall, hidden), t) for t in kinds]
        out.append(jax.ShapeDtypeStruct((tall, width), jnp.bfloat16))
        out_specs += specs(4, pltpu.VMEM)
    return pl.pallas_call(
        lambda *refs: backward_kernel(*refs, load=load, keep=keep),
        in_specs=specs(1, pltpu.SMEM) + specs(8, pltpu.VMEM) + specs(3, pltpu.HBM if load else pltpu.VMEM),
        out_specs=out_specs,
        out_shape=out,
        scratch_shapes=scratch,
        compiler_params=pltpu.CompilerParams(vmem_limit_bytes=grant(tall, width)),
        name=f"backward_{int(load)}{int(keep)}",
    )(flag, *last, *arriving, *tables, *placed(weights, load))


def member_table(onehot, table):
    return jnp.dot(onehot, table, precision=HIGH)


def member_sums(onehot, values):
    return jnp.dot(onehot.T, values, precision=HIGH)


def rows_product(left, right):
    part = lax.dot_general(
        left[...], right[...], (((0,), (0,)), ((), ())), preferred_element_type=jnp.float32
    )
    return part.astype(jnp.bfloat16)


def outer_kernel(left, right, out):
    out[...] = rows_product(left, right)


def outer_pair_kernel(left, first, second, first_out, second_out):
    first_out[...] = rows_product(left, first)
    second_out[...] = rows_product(left, second)


def outer(left, right):
    tall, height = left.shape
    width = right.shape[1]
    size = chunk_of(height)
    return pl.pallas_call(
        outer_kernel,
        grid=(height // size,),
        in_specs=[
            pl.BlockSpec((tall, size), lambda i: (0, i)),
            pl.BlockSpec((tall, width), lambda i: (0, 0)),
        ],
        out_specs=pl.BlockSpec((size, width), lambda i: (i, 0)),
        out_shape=jax.ShapeDtypeStruct((height, width), jnp.bfloat16),
        compiler_params=pltpu.CompilerParams(vmem_limit_bytes=40 << 20),
        name="outer",
    )(left, right)


def outer_pair(left, first, second):
    tall, height = left.shape
    width = first.shape[1]
    size = chunk_of(width)
    column = pl.BlockSpec((tall, size), lambda i: (0, i))
    return pl.pallas_call(
        outer_pair_kernel,
        grid=(width // size,),
        in_specs=[pl.BlockSpec((tall, height), lambda i: (0, 0)), column, column],
        out_specs=[pl.BlockSpec((height, size), lambda i: (0, i))] * 2,
        out_shape=[jax.ShapeDtypeStruct((height, width), jnp.bfloat16)] * 2,
        compiler_params=pltpu.CompilerParams(vmem_limit_bytes=40 << 20),
        name="outer_pair",
    )(left, first, second)


def on_device(
    tokens, member_ids, cotangent, w_gate, w_up, w_down, in_scale, mid_scale, out_scale, norm_gain
):
    sections = lax.axis_size("section")
    section = lax.axis_index("section")
    micro, own, width = tokens.shape
    rows = micro * own
    count = group_size()
    group = lax.axis_index("dp") * lax.axis_size("mp") + lax.axis_index("mp")
    gate_w, up_w, down_w = w_gate[0], w_up[0], w_down[0]
    in_tab, mid_tab, out_tab = in_scale[0], mid_scale[0], out_scale[0]
    gain = norm_gain[0]
    members = in_tab.shape[0]
    labels = jnp.arange(members, dtype=jnp.int32)
    owners = jnp.bitwise_xor(group, jnp.array(slot_offsets(), jnp.int32))
    by_owner = member_ids.reshape(micro, count, own).transpose(1, 0, 2).reshape(count, rows)
    ids = jnp.take(by_owner, owners, axis=0).reshape(count * rows)
    full_hot = (ids[:, None] == labels[None, :]).astype(jnp.float32)
    row_hot = full_hot[:rows]
    in_tok = member_table(full_hot, in_tab)
    out_tok = member_table(full_hot, out_tab)
    mid_tok = member_table(full_hot, mid_tab)
    own_first = tokens.reshape(rows, width)
    own_last = cotangent.reshape(rows, width)
    start_flag = (section == 0).astype(jnp.int32)[None]
    end_flag = (section == sections - 1).astype(jnp.int32)[None]
    ready = (full_hot, row_hot, in_tok, out_tok, mid_tok, own_first, own_last, start_flag, end_flag)
    full_hot, row_hot, in_tok, out_tok, mid_tok, own_first, own_last, start_flag, end_flag = (
        lax.optimization_barrier(ready)
    )
    out_rows = out_tok[:rows]
    first = spread(own_first)
    last = spread(own_last)
    gain_row = gain[None]

    at_start = start_flag[0] > 0
    arriving, part = first, own_first
    weights = (gate_w, up_w, down_w)
    turned = [None] * 3
    for step in range(sections):
        keep = step + 1 == sections
        turn = step - 1 if 0 < step <= 3 else None
        kept, sent, *found = forward_stage(
            start_flag, first, arriving, gain_row, in_tok, mid_tok, weights, step == 0, turn, keep
        )
        if step == 0:
            weights, found = found[:3], found[3:]
        if turn is not None:
            turned[turn], found = found[0], found[1:]
        if keep:
            gate_pre, up_pre, hidden, whole_scaled = found
        x_own = jnp.where(at_start, own_first, part).astype(jnp.float32)
        down_out = row_sums(kept, sent, rows)
        x_next = (x_own + down_out * out_rows).astype(jnp.bfloat16)
        if step + 1 < sections:
            arriving, part = spread_along(x_next, 1)

    turned = [w.T if t is None else t for w, t in zip((gate_w, up_w, down_w), turned)]
    inv_rms = lax.rsqrt(jnp.mean(x_own * x_own, axis=-1, keepdims=True) + EPS)
    normed = x_own * inv_rms
    in_rows = in_tok[:rows]
    product = jax.nn.silu(gate_pre) * up_pre
    sigma = jax.nn.sigmoid(gate_pre)
    silu_gate = gate_pre * sigma
    silu_grad = up_pre * sigma * (1.0 + gate_pre * (1.0 - sigma))
    tables = (out_tok, mid_tok, silu_grad, silu_gate)
    at_end = end_flag[0] > 0
    arriving, part = last, own_last
    for step in range(sections):
        keep = step + 1 == sections
        kept, sent, *found = backward_stage(end_flag, last, arriving, tables, turned, step == 0, keep)
        if step == 0:
            turned, found = found[:3], found[3:]
        if keep:
            grad_hidden, grad_gate_pre, grad_up_pre, whole_cot = found
        grad_y = jnp.where(at_end, own_last, part).astype(jnp.float32)
        grad_scaled = row_sums(kept, sent, rows)
        grad_w = grad_scaled * in_rows
        grad_normed = grad_w * gain
        grad_x = inv_rms * (
            grad_normed - normed * jnp.mean(grad_normed * normed, axis=-1, keepdims=True)
        )
        grad_input = (grad_y + grad_x).astype(jnp.bfloat16)
        if step + 1 < sections:
            arriving, part = spread_along(grad_input, -1)

    small = jnp.concatenate(
        [
            member_sums(row_hot, grad_scaled * normed * gain),
            member_sums(row_hot, grad_y * down_out),
            jnp.sum(grad_w * normed, axis=0)[None],
        ],
        0,
    )
    acc_mid = member_sums(full_hot, grad_hidden * product)
    acc_down = outer(hidden, whole_cot)
    whole_scaled, small, acc_down = lax.optimization_barrier((whole_scaled, small, acc_down))
    small = row_sums_all(small)
    acc_gate, acc_up = outer_pair(whole_scaled, grad_gate_pre, grad_up_pre)
    return (
        x_next.reshape(1, micro, own, width),
        grad_input.reshape(1, micro, own, width),
        acc_gate[None],
        acc_up[None],
        acc_down[None],
        small[None, :members],
        acc_mid[None],
        small[None, members : 2 * members],
        small[None, 2 * members],
    )


def row_sums_all(small):
    part = small.astype(jnp.bfloat16)
    part = part.astype(jnp.float32) + swapped(part, core_offset()).astype(jnp.float32)
    part = part.astype(jnp.bfloat16)
    terms = [part] + [swapped(part, j) for j in chip_offsets()[1:]]
    terms = [term.astype(jnp.float32) for term in terms]
    while len(terms) > 1:
        terms = [terms[i] + terms[i + 1] for i in range(0, len(terms), 2)]
    return terms[0]


def solution(mesh):
    in_specs = (
        P(None, ("dp", "mp"), None),
        P(),
        P(None, ("dp", "mp"), None),
        P("section", None, ("dp", "mp")),
        P("section", None, ("dp", "mp")),
        P("section", ("dp", "mp"), None),
        P("section", None, None),
        P("section", None, ("dp", "mp")),
        P("section", None, None),
        P("section", None),
    )
    out_specs = (
        P("section", None, ("dp", "mp"), None),
        P("section", None, ("dp", "mp"), None),
        P("section", None, ("dp", "mp")),
        P("section", None, ("dp", "mp")),
        P("section", ("dp", "mp"), None),
        P("section", None, None),
        P("section", None, ("dp", "mp")),
        P("section", None, None),
        P("section", None),
    )
    return jax.shard_map(
        on_device, mesh=mesh, in_specs=in_specs, out_specs=out_specs, check_vma=False
    )
```
